128 devices in a mesh: depth: 8 (over z, core), row: 16 (over x, y).
Axes of the slice: x: 4, y: 4, z: 4, core: 2. Of those that a mesh axis runs over, the one named last changes fastest.
Arguments:
- volume: float32 [256, 512, 4096], P('depth', 'row'), may hold values from 0.02 to 0.52
- palette: float32 [3, 8], replicated, may hold values from 0.15 to 4
Outputs:
- image: float32 [4, 512, 4096], P(None, 'row', 'depth')
The draws below stay inside these ranges and needn't reach their ends.
All inputs are finite; a program needn't handle non-finite values.
Results may differ from the reference program's by a relative error of at most 0.0003.
Values sent between devices are 32-bit elements; how exact they have to be, the bound alone decides.
No kernel may reach another device: no remote copies, remote signals or barrier semaphores. Data moves between devices by JAX's collectives and lax.ppermute only.
A program may use at most 192 MiB of HBM per device.

```python
import jax
import jax.numpy as jnp
from jax import lax

CY = 32
NX = 4096
J = 8
NZ = 256
NY = 512


def draw_volume(key, part):
    choose_key = jax.random.fold_in(key, 11)
    level_key = jax.random.fold_in(key, 12)
    extent = (NZ, NY, NX)
    selector = jax.random.randint(choose_key, extent, 0, 4)
    levels = jax.random.uniform(level_key, extent, jnp.float32)
    sparse = 0.02 * jnp.exp(1.3862944 * levels)
    filled = 0.5 + 0.024 * (levels - 0.5)
    return jnp.where(selector == 0, sparse, filled).astype(jnp.float32)


def draw_palette(key, part):
    weak_key = jax.random.fold_in(key, 21)
    strong_key = jax.random.fold_in(key, 22)
    weaker = jax.random.uniform(weak_key, (3, J), jnp.float32, 0.2, 0.8)
    stronger = jax.random.uniform(strong_key, (3, J), jnp.float32, 2.5, 3.5)
    column = jnp.broadcast_to(jnp.arange(J)[None, :], (3, J))
    marked = (column == 1) | (column == J - 2)
    return jnp.where(marked, stronger, weaker).astype(jnp.float32)


def setup_inputs(seed: int = 0) -> dict:
    seeds = jax.random.split(jax.random.key(seed), 3)
    return {
        "volume": draw_volume(jax.random.fold_in(seeds[2], 71), 0),
        "palette": draw_palette(jax.random.fold_in(seeds[2], 71), 0),
    }


def sample_terms(field, grad_z, grad_y, grad_x, palette, scale):
    along = 0.36 * grad_z + 0.48 * grad_y + 0.8 * grad_x
    square = grad_z * grad_z + grad_y * grad_y + grad_x * grad_x
    shade = 0.25 + 0.75 * jnp.abs(along) / jnp.sqrt(square + 0.04)
    bumps = palette.shape[1]
    colors = [jnp.zeros_like(field) for k in range(3)]
    for j in range(bumps):
        bump = jnp.exp(-jnp.square((bumps - 1) * field - j))
        for k in range(3):
            colors[k] = colors[k] + palette[k, j] * bump
    colors = [shade * c for c in colors]
    return (field * scale, colors)

def reference(volume, palette):
    depth_cells, rows, columns = volume.shape
    scale = 4.0 / NZ

    def one_block(start):
        zero = jnp.int32(0)
        middle = lax.dynamic_slice(volume, (zero, start, zero), (depth_cells, CY, columns))
        above_row = jnp.maximum(start - 1, 0).astype(jnp.int32)
        below_row = jnp.minimum(start + CY, rows - 1).astype(jnp.int32)
        above = lax.dynamic_slice(volume, (zero, above_row, zero), (depth_cells, 1, columns))
        below = lax.dynamic_slice(volume, (zero, below_row, zero), (depth_cells, 1, columns))
        above = jnp.where(start > 0, above, jnp.zeros_like(above))
        below = jnp.where(start + CY < rows, below, jnp.zeros_like(below))
        extended = jnp.concatenate([above, middle, below], axis=1)
        padded = jnp.pad(middle, ((1, 1), (0, 0), (1, 1)))
        grad_z = (padded[2:, :, 1:-1] - padded[:-2, :, 1:-1]) * 0.5
        grad_y = (extended[:, 2:, :] - extended[:, :-2, :]) * 0.5
        grad_x = (padded[1:-1, :, 2:] - padded[1:-1, :, :-2]) * 0.5
        tau, colors = sample_terms(middle, grad_z, grad_y, grad_x, palette, scale)
        before = jnp.cumsum(tau, axis=0) - tau
        weight = jnp.exp(-before) * (1.0 - jnp.exp(-tau))
        channels = [lax.optimization_barrier(jnp.sum(weight * c, axis=0)) for c in colors]
        channels.append(1.0 - jnp.exp(-lax.optimization_barrier(jnp.sum(tau, axis=0))))
        return jnp.stack(channels, axis=0)
    starts = (jnp.arange(rows // CY) * CY).astype(jnp.int32)
    blocks = lax.map(one_block, starts)
    return jnp.transpose(blocks, (1, 0, 2, 3)).reshape(4, rows, columns)
```

```python
import functools
import math

import jax
import jax.numpy as jnp
from jax import lax
from jax.experimental import pallas as pl
from jax.experimental.pallas import tpu as pltpu
from jax.sharding import PartitionSpec as P

LANES = 128
SUBLANES = 8
LOG2E = math.log2(math.e)
TO_Y = 4.0 / 3.0
TO_X = 20.0 / 9.0
AMBIENT = 0.25 / 0.27
VMEM_BYTES = 58 * 2**20


def lane_masks():
    lane = lax.broadcasted_iota(jnp.int32, (SUBLANES, LANES), 1)
    return lane == 0, lane == LANES - 1


def shade_of(dz, dy, dx):
    along = jnp.abs(dz + TO_Y * dy + TO_X * dx)
    square = (dz * dz + 0.16) + (dy * dy + dx * dx)
    return along * lax.rsqrt(square) + AMBIENT


def across(left, here, right, first, last):
    after = pltpu.roll(jnp.where(first, right, here), LANES - 1, 1)
    before = pltpu.roll(jnp.where(last, left, here), 1, 1)
    return after - before


def add_bumps(moments, amount, field):
    ratio = jnp.exp2(field * (14 * LOG2E))
    amount = amount * jnp.exp2(field * field * (-49 * LOG2E))
    out = []
    for j, moment in enumerate(moments):
        out.append(amount if moment is None else moment + amount)
        if j + 1 < len(moments):
            amount = amount * ratio
    return out


def coefficients(palette_ref):
    bumps = palette_ref.shape[1]
    return [[palette_ref[k, j] * jnp.float32(0.27 * math.exp(-j * j)) for j in range(bumps)] for k in range(3)]


def contracted(coef, moments):
    out = []
    for k in range(3):
        total = moments[0] * coef[k][0]
        for j in range(1, len(moments)):
            total = total + moments[j] * coef[k][j]
        out.append(total)
    return out


def sample_kernel(volume_ref, prev_ref, next_ref, edge_ref, early_ref, palette_ref, *refs, mode, scale, depth):
    planes, rows, columns = volume_ref.shape
    tiles = columns // LANES
    if mode == "A":
        out_ref, vb, sem = refs
    elif mode == "B":
        keep_ref, send_ref, vb, vs, sem, sem_s = refs
    else:
        keep_ref, send_ref, vb, sem = refs
    first_row, count, at = {"A": (0, 24, 0), "B": (8, 24, 0), "C": (0, 16, 8), "D": (16, 16, 0)}[mode]
    mid = pl.ds(SUBLANES, SUBLANES)

    def tile_lanes(c):
        return pl.ds(pl.multiple_of(c * LANES, LANES), LANES)

    def copies(c):
        out = [
            pltpu.make_async_copy(
                volume_ref.at[:, pl.ds(first_row, count), tile_lanes(c)],
                vb.at[c + 1, :, pl.ds(at, count), :],
                sem.at[c],
            )
        ]
        if mode == "B":
            for i, z in enumerate((0, planes - 1)):
                out.append(
                    pltpu.make_async_copy(
                        volume_ref.at[z, pl.ds(0, 24), tile_lanes(c)],
                        vs.at[c + 1, i],
                        sem_s.at[c, i],
                    )
                )
        return out

    def begin(c, _):
        for copy in copies(c):
            copy.start()
        return 0

    lax.fori_loop(0, tiles, begin, 0)
    zero = jnp.zeros((planes, SUBLANES, LANES), jnp.float32)
    for c in (0, tiles + 1):
        vb[c, :, 8:16, :] = zero
        if mode == "B":
            vs[c, :, 8:16, :] = zero[:2]
    if mode in "CD":
        row = 7 if mode == "C" else 16

        def place(c, _):
            for z in range(planes):
                vb[c + 1, z, row : row + 1, :] = edge_ref[z : z + 1, tile_lanes(c)]
            return 0

        lax.fori_loop(0, tiles, place, 0)
    first, last = lane_masks()
    coef = coefficients(palette_ref)
    core = lax.axis_index(depth) % 2
    for copy in copies(0):
        copy.wait()

    def store(c, values, where):
        block = c // (tiles // 8)
        at_lane = pl.ds(pl.multiple_of((block // 2) * (columns // 8) + (c % (tiles // 8)) * LANES, LANES), LANES)

        @pl.when(block % 2 == core)
        def _():
            for k, value in enumerate(values):
                keep_ref[k, where, at_lane] = value

        @pl.when(block % 2 != core)
        def _():
            for k, value in enumerate(values):
                send_ref[k, where, at_lane] = value

    main_row = {"A": 8, "B": 16, "C": 0, "D": 24}[mode]
    inner = mode == "A"

    def body(c, _):
        @pl.when(c < tiles - 1)
        def _():
            for copy in copies(c + 1):
                copy.wait()

        moments = [None] * 8
        total = jnp.zeros((SUBLANES, LANES), jnp.float32)
        passed = jnp.ones((SUBLANES, LANES), jnp.float32)
        for z in range(planes):
            here = vb[c + 1, z, mid, :]
            total = total + here
            after = jnp.exp2(total * (-scale * LOG2E))
            if not (inner and z in (0, planes - 1)):
                up = vb[c + 1, z + 1, mid, :] if z < planes - 1 else next_ref[pl.ds(main_row, 8), tile_lanes(c)]
                down = vb[c + 1, z - 1, mid, :] if z > 0 else prev_ref[pl.ds(main_row, 8), tile_lanes(c)]
                dy = vb[c + 1, z, pl.ds(9, 8), :] - vb[c + 1, z, pl.ds(7, 8), :]
                dx = across(vb[c, z, mid, :], here, vb[c + 2, z, mid, :], first, last)
                moments = add_bumps(moments, (passed - after) * shade_of(up - down, dy, dx), here)
            passed = after
        colors = contracted(coef, moments)
        if mode == "A":
            for k in range(3):
                out_ref[k, :, tile_lanes(c)] = colors[k]
            out_ref[3, :, tile_lanes(c)] = passed
            return 0
        if mode == "B":
            store(c, colors + [passed], pl.ds(8, 8))
            moments = [None] * 8
            passed = early_ref[3, :, tile_lanes(c)]
            for i, z in enumerate((0, planes - 1)):
                here = vs[c + 1, i, mid, :]
                up = vb[c + 1, 1, pl.ds(0, 8), :] if i == 0 else next_ref[pl.ds(8, 8), tile_lanes(c)]
                down = prev_ref[pl.ds(8, 8), tile_lanes(c)] if i == 0 else vb[c + 1, planes - 2, pl.ds(0, 8), :]
                dy = vs[c + 1, i, pl.ds(9, 8), :] - vs[c + 1, i, pl.ds(7, 8), :]
                dx = across(vs[c, i, mid, :], here, vs[c + 2, i, mid, :], first, last)
                if i == 0:
                    amount = 1.0 - jnp.exp2(here * (-scale * LOG2E))
                else:
                    amount = passed * (jnp.exp2(here * (scale * LOG2E)) - 1.0)
                moments = add_bumps(moments, amount * shade_of(up - down, dy, dx), here)
            colors = contracted(coef, moments)
            colors = [early_ref[k, :, tile_lanes(c)] + colors[k] for k in range(3)]
            store(c, colors + [passed], pl.ds(0, 8))
            return 0
        store(c, colors + [passed], pl.ds(0, 8))
        return 0

    lax.fori_loop(0, tiles, body, 0)


def sample(mode, volume, before, after, edge, early, palette, scale, depth):
    planes, rows, columns = volume.shape
    tiles = columns // LANES
    vmem = pl.BlockSpec(memory_space=pltpu.VMEM)
    scratch = [pltpu.VMEM((tiles + 2, planes, 24, LANES), jnp.float32)]
    if mode == "B":
        scratch.append(pltpu.VMEM((tiles + 2, 2, 24, LANES), jnp.float32))
    scratch.append(pltpu.SemaphoreType.DMA((tiles,)))
    if mode == "B":
        scratch.append(pltpu.SemaphoreType.DMA((tiles, 2)))
    if mode == "A":
        out_shape = jax.ShapeDtypeStruct((4, 8, columns), jnp.float32)
        out_specs = vmem
    else:
        half = jax.ShapeDtypeStruct((4, 16 if mode == "B" else 8, columns // 2), jnp.float32)
        out_shape = (half, half)
        out_specs = (vmem, vmem)
    given = [volume, before, after, edge, early, palette]
    specs = [pl.BlockSpec(memory_space=pl.ANY)] + [vmem] * 4 + [pl.BlockSpec(memory_space=pltpu.SMEM)]
    used = [value is not None for value in given]

    def kernel(*refs):
        refs = list(refs)
        full = [refs.pop(0) if there else None for there in used]
        sample_kernel(*full, *refs, mode=mode, scale=scale, depth=depth)

    return pl.pallas_call(
        kernel,
        out_shape=out_shape,
        in_specs=[spec for spec, there in zip(specs, used) if there],
        out_specs=out_specs,
        scratch_shapes=scratch,
        compiler_params=pltpu.CompilerParams(vmem_limit_bytes=VMEM_BYTES),
        name="sample_" + mode,
    )(*[value for value in given if value is not None])


def merge_kernel(keep_ref, arrived_ref, *out_refs, depth):
    index = lax.axis_index(depth)
    chip = index // 2
    width = out_refs[0].shape[2]
    for core in range(2):
        front, back = (keep_ref, arrived_ref) if core == 0 else (arrived_ref, keep_ref)

        @pl.when(index % 2 == core)
        def _():
            for step, out_ref in enumerate(out_refs):
                lanes = pl.ds(pl.multiple_of(((chip + step) % 4) * width, width), width)
                passed = front[3, :, lanes]
                for k in range(3):
                    out_ref[k] = front[k, :, lanes] + passed * back[k, :, lanes]
                out_ref[3] = passed * back[3, :, lanes]


def merge(keep, arrived, depth):
    channels, rows, columns = keep.shape
    piece = jax.ShapeDtypeStruct((channels, rows, columns // 4), jnp.float32)
    return pl.pallas_call(
        functools.partial(merge_kernel, depth=depth),
        out_shape=(piece,) * 4,
        name="merge",
    )(keep, arrived)


def final_kernel(*refs, spans, depth):
    out_ref = refs[-1]
    chip = lax.axis_index(depth) // 2
    for mine in range(4):

        @pl.when(chip == mine)
        def _():
            for i, (row, count) in enumerate(spans):
                pieces = [refs[4 * i + (mine - z) % 4] for z in range(4)]
                passed = pieces[0][3]
                colors = [pieces[0][k] for k in range(3)]
                for piece in pieces[1:]:
                    for k in range(3):
                        colors[k] = colors[k] + passed * piece[k]
                    passed = passed * piece[3]
                for k in range(3):
                    out_ref[k, row : row + count, :] = colors[k]
                out_ref[3, row : row + count, :] = 1.0 - passed


def on_device(volume, palette):
    planes, rows, columns = volume.shape
    groups = lax.axis_size("depth")
    stacks = lax.axis_size("row")
    scale = 4.0 / (planes * groups)

    def shifted(value, axis, count, step):
        pairs = [(i, i + step) for i in range(count) if 0 <= i + step < count]
        return lax.ppermute(value, axis, pairs)

    before = shifted(volume[-1], "depth", groups, 1)
    after = shifted(volume[0], "depth", groups, -1)
    above = shifted(volume[:, -1, :], "row", stacks, 1)
    below = shifted(volume[:, 0, :], "row", stacks, -1)

    run = functools.partial(sample, scale=scale, depth="depth", palette=palette)
    early = run("A", volume, None, None, None, None)
    chunks = [
        (8, 16, run("B", volume, before, after, None, early)),
        (0, 8, run("C", volume, before, after, above, None)),
        (24, 8, run("D", volume, before, after, below, None)),
    ]
    pieces = []
    for _, _, (keep, send) in chunks:
        arrived = lax.ppermute(send, "depth", [(i, i ^ 1) for i in range(groups)])
        parts = merge(keep, arrived, "depth")
        for step in range(4):
            if step == 0:
                pieces.append(parts[0])
            else:
                pairs = [(i, (i + 2 * step) % groups) for i in range(groups)]
                pieces.append(lax.ppermute(parts[step], "depth", pairs))
    spans = [(row, count) for row, count, _ in chunks]
    return pl.pallas_call(
        functools.partial(final_kernel, spans=spans, depth="depth"),
        out_shape=jax.ShapeDtypeStruct((4, rows, columns // groups), jnp.float32),
        name="final",
    )(*pieces)


def solution(mesh):
    return jax.shard_map(
        on_device,
        mesh=mesh,
        in_specs=(P("depth", "row", None), P()),
        out_specs=P(None, "row", "depth"),
        check_vma=False,
    )
```

```python
import functools
import math

import jax
import jax.numpy as jnp
from jax import lax
from jax.experimental import pallas as pl
from jax.experimental.pallas import tpu as pltpu
from jax.sharding import PartitionSpec as P


LANES = 128
SUBLANES = 8
BELOW = 8
STAGED = 48
LOG2E = math.log2(math.e)
TO_Y = 4.0 / 3.0
TO_X = 20.0 / 9.0
AMBIENT = 0.25 / 0.27
AHEAD = 4
SPLIT = 20
VMEM = pl.BlockSpec(memory_space=pltpu.VMEM)
ANY = pl.BlockSpec(memory_space=pl.ANY)
HBM = pl.BlockSpec(memory_space=pltpu.HBM)
SMEM = pl.BlockSpec(memory_space=pltpu.SMEM)


def in_vmem(value):
    return pltpu.with_memory_space_constraint(value, pltpu.VMEM)


def vmem_shape(*shape):
    return pltpu.VMEM(shape, jnp.float32)


def shade_of(dz, dy, dx):
    along = jnp.abs(dz + TO_Y * dy + TO_X * dx)
    square = (dz * dz + 0.16) + (dy * dy + dx * dx)
    return along * lax.rsqrt(square) + AMBIENT


def across(left, here, right):
    lane = lax.broadcasted_iota(jnp.int32, (SUBLANES, LANES), 1)
    after = pltpu.roll(jnp.where(lane == 0, right, here), LANES - 1, 1)
    before = pltpu.roll(jnp.where(lane == LANES - 1, left, here), 1, 1)
    return after - before


def add_bumps(moments, amount, field):
    ratio = jnp.exp2(field * (14 * LOG2E))
    amount = amount * jnp.exp2(field * field * (-49 * LOG2E))
    out = []
    for j, moment in enumerate(moments):
        out.append(amount if moment is None else moment + amount)
        if j + 1 < len(moments):
            amount = amount * ratio
    return out


def coefficients(palette_ref):
    bumps = palette_ref.shape[1]
    return [[palette_ref[k, j] * jnp.float32(0.27 * math.exp(-j * j)) for j in range(bumps)] for k in range(3)]


def contracted(coef, moments):
    out = []
    for k in range(3):
        total = moments[0] * coef[k][0]
        for j in range(1, len(moments)):
            total = total + moments[j] * coef[k][j]
        out.append(total)
    return out


def tile_lanes(c):
    return pl.ds(pl.multiple_of(c * LANES, LANES), LANES)


def gradients(vb, c, z, row, up, down):
    here = vb[c + 1, z, pl.ds(row, 8), :]
    dy = vb[c + 1, z, pl.ds(row + 1, 8), :] - vb[c + 1, z, pl.ds(row - 1, 8), :]
    dx = across(vb[c, z, pl.ds(row, 8), :], here, vb[c + 2, z, pl.ds(row, 8), :])
    if up is None:
        up = vb[c + 1, z + 1, pl.ds(row, 8), :]
    if down is None:
        down = vb[c + 1, z - 1, pl.ds(row, 8), :]
    return here, up - down, dy, dx


def march(vb, c, group, planes, scale, ends=None):
    row = BELOW + group * SUBLANES
    moments = [None] * 8
    total = jnp.zeros((SUBLANES, LANES), jnp.float32)
    passed = jnp.ones((SUBLANES, LANES), jnp.float32)
    for z in range(planes):
        outer = z in (0, planes - 1)
        total = total + vb[c + 1, z, pl.ds(row, 8), :]
        after = jnp.exp2(total * (-scale * LOG2E))
        if not outer or ends is not None:
            down = ends[0] if z == 0 else None
            up = ends[1] if z == planes - 1 else None
            here, dz, dy, dx = gradients(vb, c, z, row, up, down)
            moments = add_bumps(moments, (passed - after) * shade_of(dz, dy, dx), here)
        passed = after
    return moments, passed


def march_ends(vb, c, group, planes, scale, ends, passed):
    row = BELOW + group * SUBLANES
    here, dz, dy, dx = gradients(vb, c, 0, row, None, ends[0])
    amount = 1.0 - jnp.exp2(here * (-scale * LOG2E))
    moments = add_bumps([None] * 8, amount * shade_of(dz, dy, dx), here)
    here, dz, dy, dx = gradients(vb, c, planes - 1, row, ends[1], None)
    amount = passed * (jnp.exp2(here * (scale * LOG2E)) - 1.0)
    return add_bumps(moments, amount * shade_of(dz, dy, dx), here)


def stage_kernel(volume_ref, palette_ref, vb, early_ref, top_ref, bottom_ref, sem, *, scale):
    planes, rows, columns = volume_ref.shape
    tiles = columns // LANES

    def copy(c):
        return pltpu.make_async_copy(
            volume_ref.at[:, :, tile_lanes(c)], vb.at[c + 1, :, pl.ds(BELOW, rows), :], sem.at[c]
        )

    for c in range(AHEAD):
        copy(c).start()
    zero = jnp.zeros((planes, rows, LANES), jnp.float32)
    vb[0, :, BELOW : BELOW + rows, :] = zero
    vb[tiles + 1, :, BELOW : BELOW + rows, :] = zero
    coef = coefficients(palette_ref)

    def arrive(c):
        copy(c).wait()

        @pl.when(c + AHEAD < tiles)
        def _():
            copy(c + AHEAD).start()

        flat = vb.reshape(tiles + 2, planes * STAGED, LANES)
        for z in range(0, planes, 8):
            for out, row in ((top_ref, BELOW), (bottom_ref, BELOW + rows - 1)):
                out[z : z + 8, tile_lanes(c)] = flat[c + 1, pl.ds(z * STAGED + row, 8, stride=STAGED), :]

    arrive(0)

    def body(c, _):
        arrive(c + 1)
        moments, passed = march(vb, c, 1, planes, scale)
        for k, value in enumerate(contracted(coef, moments) + [passed]):
            early_ref[k, :, tile_lanes(c)] = value
        return 0

    lax.fori_loop(0, SPLIT, body, 0)

    def rest(c, _):
        arrive(c)
        return 0

    lax.fori_loop(SPLIT + 1, tiles, rest, 0)


def early_kernel(vb, palette_ref, early_ref, *, scale, planes):
    tiles = vb.shape[0] - 2
    coef = coefficients(palette_ref)

    def body(c, _):
        moments, passed = march(vb, c, 1, planes, scale)
        for k, value in enumerate(contracted(coef, moments) + [passed]):
            early_ref[k, :, tile_lanes(c)] = value
        return 0

    lax.fori_loop(SPLIT, tiles, body, 0)


def place_of(block):
    chip = block // 2
    return 2 * ((chip ^ (chip // 2)) % 2) + chip // 2


def store_halves(keep_ref, send_ref, c, tiles, index, values, rows):
    per_block = tiles // 8
    block = c // per_block
    lanes = tile_lanes(place_of(block) * per_block + c % per_block)

    @pl.when(block % 2 == index % 2)
    def _():
        for k, value in enumerate(values):
            keep_ref[k, rows, lanes] = value

    @pl.when(block % 2 != index % 2)
    def _():
        for k, value in enumerate(values):
            send_ref[k, rows, lanes] = value


def depth_ends(prev_ref, next_ref, index, groups):
    inside_prev = jnp.where(index == 0, 0.0, 1.0)
    inside_next = jnp.where(index == groups - 1, 0.0, 1.0)

    def ends(c, group):
        rows = pl.ds(group * SUBLANES, SUBLANES)
        return prev_ref[rows, tile_lanes(c)] * inside_prev, next_ref[rows, tile_lanes(c)] * inside_next

    return ends


def middle_kernel(vb, prev_ref, next_ref, first_ref, second_ref, palette_ref, keep_ref, send_ref, *, scale, planes, depth, groups):
    tiles = vb.shape[0] - 2
    coef = coefficients(palette_ref)
    index = lax.axis_index(depth)
    ends = depth_ends(prev_ref, next_ref, index, groups)

    def body(c, _):
        moments, passed = march(vb, c, 2, planes, scale, ends(c, 2))
        store_halves(keep_ref, send_ref, c, tiles, index, contracted(coef, moments) + [passed], pl.ds(8, 8))
        early = [jnp.where(c < SPLIT, first_ref[k, :, tile_lanes(c)], second_ref[k, :, tile_lanes(c)]) for k in range(4)]
        moments = march_ends(vb, c, 1, planes, scale, ends(c, 1), early[3])
        colors = [early[k] + color for k, color in enumerate(contracted(coef, moments))]
        store_halves(keep_ref, send_ref, c, tiles, index, colors + [early[3]], pl.ds(0, 8))
        return 0

    lax.fori_loop(0, tiles, body, 0)


def outer_kernel(vb_in, prev_ref, next_ref, edge_ref, after_ref, palette_ref, vb, keep_ref, send_ref, *, scale, planes, depth, groups, row, stacks, top):
    tiles = vb.shape[0] - 2
    coef = coefficients(palette_ref)
    index = lax.axis_index(depth)
    ends = depth_ends(prev_ref, next_ref, index, groups)
    at_end = lax.axis_index(row) == (0 if top else stacks - 1)
    inside = jnp.where(at_end, 0.0, 1.0)
    group = 0 if top else 3
    slot = BELOW - 1 if top else BELOW + 4 * SUBLANES
    flat = vb.reshape(tiles + 2, planes * STAGED, LANES)

    def place(c, _):
        for z in range(0, planes, 8):
            flat[c + 1, pl.ds(z * STAGED + slot, 8, stride=STAGED), :] = edge_ref[z : z + 8, tile_lanes(c)] * inside
        return 0

    lax.fori_loop(0, tiles, place, 0)

    def body(c, _):
        moments, passed = march(vb, c, group, planes, scale, ends(c, group))
        store_halves(keep_ref, send_ref, c, tiles, index, contracted(coef, moments) + [passed], pl.ds(0, 8))
        return 0

    lax.fori_loop(0, tiles, body, 0)


def blend(front, back, lanes):
    passed = front[3, :, lanes]
    out = [front[k, :, lanes] + passed * back[k, :, lanes] for k in range(3)]
    return out + [passed * back[3, :, lanes]]


def merge_kernel(mine_ref, theirs_ref, keep_ref, send_ref, *, depth, step):
    index = lax.axis_index(depth)
    chip = index // 2
    width = keep_ref.shape[2]
    if step == 0:
        in_front, half = index % 2 == 0, (chip ^ (chip // 2)) % 2
    else:
        in_front, half = chip % 2 == 0, chip // 2
    keep_lanes = pl.ds(pl.multiple_of(half * width, width), width)
    send_lanes = pl.ds(pl.multiple_of((1 - half) * width, width), width)
    for mine_first in (True, False):

        @pl.when(in_front == mine_first)
        def _():
            front, back = (mine_ref, theirs_ref) if mine_first else (theirs_ref, mine_ref)
            for out_ref, lanes in ((send_ref, send_lanes), (keep_ref, keep_lanes)):
                for k, value in enumerate(blend(front, back, lanes)):
                    out_ref[k] = value


def final_kernel(*refs, spans, depth):
    out_ref = refs[-1]
    chip = lax.axis_index(depth) // 2
    for mine_first in (True, False):

        @pl.when((chip < 2) == mine_first)
        def _():
            for i, (row, count) in enumerate(spans):
                front, back = (refs[2 * i], refs[2 * i + 1]) if mine_first else (refs[2 * i + 1], refs[2 * i])
                values = blend(front, back, slice(None))
                for k in range(3):
                    out_ref[k, row : row + count, :] = values[k]
                out_ref[3, row : row + count, :] = 1.0 - values[3]


def call(body, out_shape, in_specs, args, scratch=(), aliases=None, limit=4, **kwargs):
    single = not isinstance(out_shape, tuple)
    out_specs = VMEM if single else (VMEM,) * len(out_shape)
    return pl.pallas_call(
        functools.partial(body, **kwargs),
        out_shape=out_shape,
        in_specs=in_specs,
        out_specs=out_specs,
        scratch_shapes=scratch,
        input_output_aliases=aliases or {},
        compiler_params=pltpu.CompilerParams(vmem_limit_bytes=limit * 2**20),
    )(*args)


def on_device(volume, palette):
    planes, rows, columns = volume.shape
    groups = lax.axis_size("depth")
    stacks = lax.axis_size("row")
    tiles = columns // LANES
    scale = 4.0 / (planes * groups)

    def ring(value, axis, count, step):
        return lax.ppermute(value, axis, [(i, (i + step) % count) for i in range(count)])

    before = ring(volume[-1], "depth", groups, 1)
    after = ring(volume[0], "depth", groups, -1)
    staged = vmem_shape(tiles + 2, planes, STAGED, LANES)
    strip = vmem_shape(4, SUBLANES, columns)
    edge = vmem_shape(planes, columns)
    vb, first, top, bottom = call(
        stage_kernel,
        (staged, strip, edge, edge),
        [HBM, SMEM],
        (pltpu.with_memory_space_constraint(volume, pltpu.HBM), palette),
        scratch=[pltpu.SemaphoreType.DMA((tiles,))],
        scale=scale,
    )
    above = ring(bottom, "row", stacks, 1)
    below = ring(top, "row", stacks, -1)
    common = dict(scale=scale, planes=planes)
    second = call(early_kernel, strip, [VMEM, SMEM], (in_vmem(vb), palette), **common)
    common.update(depth="depth", groups=groups)
    before, after = in_vmem(before), in_vmem(after)
    half = lambda count: (vmem_shape(4, count, columns // 2),) * 2
    keep, send = call(
        middle_kernel,
        half(16),
        [VMEM] * 5 + [SMEM],
        (in_vmem(vb), before, after, in_vmem(first), in_vmem(second), palette),
        **common,
    )
    pairs = lambda other: [(i, other(i)) for i in range(groups)]
    partners = [pairs(lambda i: i ^ 1), pairs(lambda i: i ^ 2), pairs(lambda i: groups - 2 - i // 2 * 2 + i % 2)]

    def outer(vb, edge, behind, top):
        return call(
            outer_kernel,
            (staged,) + half(8),
            [VMEM] * 4 + [ANY, SMEM],
            (in_vmem(vb), before, after, in_vmem(edge), behind, palette),
            aliases={0: 0},
            row="row",
            stacks=stacks,
            top=top,
            **common,
        )

    def swap(value, step):
        return lax.ppermute(value, "depth", partners[step])

    def merged(keep, arrived, step):
        channels, count, width = keep.shape
        shape = (vmem_shape(channels, count, width // 2),) * 2
        return call(merge_kernel, shape, [VMEM, VMEM], (in_vmem(keep), in_vmem(arrived)), depth="depth", step=step)

    kept = [keep, None, None]
    arrived = [swap(send, 0), None, None]
    vb, kept[1], send = outer(vb, above, kept[0], True)
    arrived[1] = swap(send, 0)
    kept[0], send = merged(kept[0], arrived[0], 0)
    arrived[0] = swap(send, 1)
    vb, kept[2], send = outer(vb, below, kept[0], False)
    arrived[2] = swap(send, 0)
    kept[0], send = merged(kept[0], arrived[0], 1)
    arrived[0] = swap(send, 2)
    for i in (1, 2):
        kept[i], send = merged(kept[i], arrived[i], 0)
        arrived[i] = swap(send, 1)
    for i in (1, 2):
        kept[i], send = merged(kept[i], arrived[i], 1)
        arrived[i] = swap(send, 2)
    args = []
    for i in range(3):
        args += [in_vmem(kept[i]), in_vmem(arrived[i])]
    return call(
        final_kernel,
        jax.ShapeDtypeStruct((4, rows, columns // groups), jnp.float32),
        [VMEM] * 6,
        args,
        spans=((8, 16), (0, 8), (24, 8)),
        depth="depth",
    )


def solution(mesh):
    return jax.shard_map(
        on_device,
        mesh=mesh,
        in_specs=(P("depth", "row", None), P()),
        out_specs=P(None, "row", "depth"),
        check_vma=False,
    )
```

```python
import functools
import math

import jax
import jax.numpy as jnp
from jax import lax
from jax.experimental import pallas as pl
from jax.experimental.pallas import tpu as pltpu
from jax.sharding import PartitionSpec as P


LANES = 128
SUBLANES = 8
BELOW = 8
STAGED = 48
LOG2E = math.log2(math.e)
TO_Y = 4.0 / 3.0
TO_X = 20.0 / 9.0
AMBIENT = 0.25 / 0.27
AHEAD = 10
SPLIT = 20
VMEM = pl.BlockSpec(memory_space=pltpu.VMEM)
ANY = pl.BlockSpec(memory_space=pl.ANY)
HBM = pl.BlockSpec(memory_space=pltpu.HBM)
SMEM = pl.BlockSpec(memory_space=pltpu.SMEM)


def in_vmem(value):
    return pltpu.with_memory_space_constraint(value, pltpu.VMEM)


def vmem_shape(*shape):
    return pltpu.VMEM(shape, jnp.float32)


def shade_of(dz, dy, dx):
    along = jnp.abs(dz + TO_Y * dy + TO_X * dx)
    square = (dz * dz + 0.16) + (dy * dy + dx * dx)
    return along * lax.rsqrt(square) + AMBIENT


def across(left, here, right):
    lane = lax.broadcasted_iota(jnp.int32, (SUBLANES, LANES), 1)
    after = pltpu.roll(jnp.where(lane == 0, right, here), LANES - 1, 1)
    before = pltpu.roll(jnp.where(lane == LANES - 1, left, here), 1, 1)
    return after - before


def add_bumps(moments, amount, field):
    ratio = jnp.exp2(field * (14 * LOG2E))
    amount = amount * jnp.exp2(field * field * (-49 * LOG2E))
    out = []
    for j, moment in enumerate(moments):
        out.append(amount if moment is None else moment + amount)
        if j + 1 < len(moments):
            amount = amount * ratio
    return out


def contracted(coef_ref, moments):
    bumps = len(moments)
    out = []
    for k in range(3):
        total = moments[0] * coef_ref[k * bumps]
        for j in range(1, bumps):
            total = total + moments[j] * coef_ref[k * bumps + j]
        out.append(total)
    return out


def tile_lanes(c):
    return pl.ds(pl.multiple_of(c * LANES, LANES), LANES)


def gradients(vb, c, z, row, up, down):
    here = vb[c + 1, z, pl.ds(row, 8), :]
    dy = vb[c + 1, z, pl.ds(row + 1, 8), :] - vb[c + 1, z, pl.ds(row - 1, 8), :]
    dx = across(vb[c, z, pl.ds(row, 8), :], here, vb[c + 2, z, pl.ds(row, 8), :])
    if up is None:
        up = vb[c + 1, z + 1, pl.ds(row, 8), :]
    if down is None:
        down = vb[c + 1, z - 1, pl.ds(row, 8), :]
    return here, up - down, dy, dx


def march(vb, c, group, planes, scale, ends=None):
    row = BELOW + group * SUBLANES
    moments = [None] * 8
    total = jnp.zeros((SUBLANES, LANES), jnp.float32)
    passed = jnp.ones((SUBLANES, LANES), jnp.float32)
    for z in range(planes):
        outer = z in (0, planes - 1)
        total = total + vb[c + 1, z, pl.ds(row, 8), :]
        after = jnp.exp2(total * (-scale * LOG2E))
        if not outer or ends is not None:
            down = ends[0] if z == 0 else None
            up = ends[1] if z == planes - 1 else None
            here, dz, dy, dx = gradients(vb, c, z, row, up, down)
            moments = add_bumps(moments, (passed - after) * shade_of(dz, dy, dx), here)
        passed = after
    return moments, passed


def march_ends(vb, c, group, planes, scale, ends, passed):
    row = BELOW + group * SUBLANES
    here, dz, dy, dx = gradients(vb, c, 0, row, None, ends[0])
    amount = 1.0 - jnp.exp2(here * (-scale * LOG2E))
    moments = add_bumps([None] * 8, amount * shade_of(dz, dy, dx), here)
    here, dz, dy, dx = gradients(vb, c, planes - 1, row, ends[1], None)
    amount = passed * (jnp.exp2(here * (scale * LOG2E)) - 1.0)
    return add_bumps(moments, amount * shade_of(dz, dy, dx), here)


def march_early(vb, coef_ref, early_ref, c, planes, scale):
    moments, passed = march(vb, c, 1, planes, scale)
    for k, value in enumerate(contracted(coef_ref, moments) + [passed]):
        early_ref[k, :, tile_lanes(c)] = value


def stage_kernel(volume_ref, palette_ref, vb, coef_ref, early_ref, top_ref, bottom_ref, palette, sem, palette_sem, *, scale):
    planes, rows, columns = volume_ref.shape
    tiles = columns // LANES
    bumps = palette_ref.shape[1]
    flat = vb.reshape(tiles + 2, planes * STAGED, LANES)

    def copy(c):
        return pltpu.make_async_copy(
            volume_ref.at[:, :, tile_lanes(c)], vb.at[c + 1, :, pl.ds(BELOW, rows), :], sem.at[c]
        )

    weights = pltpu.make_async_copy(palette_ref, palette, palette_sem)
    weights.start()
    for c in range(AHEAD):
        copy(c).start()
    zero = jnp.zeros((planes, rows, LANES), jnp.float32)
    vb[0, :, BELOW : BELOW + rows, :] = zero
    vb[tiles + 1, :, BELOW : BELOW + rows, :] = zero
    weights.wait()
    for k in range(3):
        for j in range(bumps):
            weight = palette[k, j] * jnp.float32(0.27 * math.exp(-j * j))
            coef_ref[k * bumps + j] = jnp.full((SUBLANES, LANES), weight, jnp.float32)

    def arrive(c):
        copy(c).wait()

        @pl.when(c + AHEAD < tiles)
        def _():
            copy(c + AHEAD).start()

        for z in range(0, planes, 8):
            for out, row in ((top_ref, BELOW), (bottom_ref, BELOW + rows - 1)):
                out[z : z + 8, tile_lanes(c)] = flat[c + 1, pl.ds(z * STAGED + row, 8, stride=STAGED), :]

    arrive(0)

    def body(i, _):
        arrive(2 * i + 1)
        arrive(2 * i + 2)
        for c in (2 * i, 2 * i + 1):
            march_early(vb, coef_ref, early_ref, c, planes, scale)
        return 0

    lax.fori_loop(0, SPLIT // 2, body, 0)

    def rest(c, _):
        arrive(c)
        return 0

    lax.fori_loop(SPLIT + 1, tiles, rest, 0)


def early_kernel(vb, coef_ref, early_ref, *, scale, planes):
    tiles = vb.shape[0] - 2

    def body(i, _):
        for c in (2 * i, 2 * i + 1):
            march_early(vb, coef_ref, early_ref, c, planes, scale)
        return 0

    lax.fori_loop(SPLIT // 2, tiles // 2, body, 0)


def place_of(block):
    chip = block // 2
    return 2 * ((chip ^ (chip // 2)) % 2) + chip // 2


def half_tiles(m, tiles, parity, unroll):
    per_block = tiles // 8
    out = []
    for i in range(unroll):
        at = m * unroll + i
        block = 2 * (at // per_block) + parity
        out.append((block * per_block + at % per_block, place_of(block) * per_block + at % per_block))
    return out


def depth_ends(prev_ref, next_ref, index, groups):
    inside_prev = jnp.where(index == 0, 0.0, 1.0)
    inside_next = jnp.where(index == groups - 1, 0.0, 1.0)

    def ends(c, group):
        rows = pl.ds(group * SUBLANES, SUBLANES)
        return prev_ref[rows, tile_lanes(c)] * inside_prev, next_ref[rows, tile_lanes(c)] * inside_next

    return ends


def middle_kernel(vb, prev_ref, next_ref, first_ref, second_ref, coef_ref, out_ref, *, scale, planes, depth, groups, send):
    tiles = vb.shape[0] - 2
    index = lax.axis_index(depth)
    ends = depth_ends(prev_ref, next_ref, index, groups)
    parity = (index + send) % 2

    def body(m, _):
        for c, place in half_tiles(m, tiles, parity, 2):
            moments, passed = march(vb, c, 2, planes, scale, ends(c, 2))
            for k, value in enumerate(contracted(coef_ref, moments) + [passed]):
                out_ref[k, 8:16, tile_lanes(place)] = value
            early = [
                jnp.where(c < SPLIT, first_ref[k, :, tile_lanes(c)], second_ref[k, :, tile_lanes(c)]) for k in range(4)
            ]
            moments = march_ends(vb, c, 1, planes, scale, ends(c, 1), early[3])
            for k, color in enumerate(contracted(coef_ref, moments)):
                out_ref[k, 0:8, tile_lanes(place)] = early[k] + color
            out_ref[3, 0:8, tile_lanes(place)] = early[3]
        return 0

    lax.fori_loop(0, tiles // 4, body, 0)


def outer_tiles(vb, prev_ref, next_ref, coef_ref, out_ref, *, scale, planes, depth, groups, send, group):
    tiles = vb.shape[0] - 2
    index = lax.axis_index(depth)
    ends = depth_ends(prev_ref, next_ref, index, groups)
    parity = (index + send) % 2

    def body(m, _):
        for c, place in half_tiles(m, tiles, parity, 2):
            moments, passed = march(vb, c, group, planes, scale, ends(c, group))
            for k, value in enumerate(contracted(coef_ref, moments) + [passed]):
                out_ref[k, :, tile_lanes(place)] = value
        return 0

    lax.fori_loop(0, tiles // 4, body, 0)


def outer_kernel(vb_in, prev_ref, next_ref, edge_ref, behind_ref, coef_ref, vb, out_ref, *, row, stacks, group, **kwargs):
    tiles, planes = vb.shape[0] - 2, vb.shape[1]
    top = group == 0
    at_end = lax.axis_index(row) == (0 if top else stacks - 1)
    inside = jnp.where(at_end, 0.0, 1.0)
    slot = BELOW - 1 if top else BELOW + 4 * SUBLANES
    flat = vb.reshape(tiles + 2, planes * STAGED, LANES)

    def place(c, _):
        for z in range(0, planes, 8):
            flat[c + 1, pl.ds(z * STAGED + slot, 8, stride=STAGED), :] = edge_ref[z : z + 8, tile_lanes(c)] * inside
        return 0

    lax.fori_loop(0, tiles, place, 0)
    outer_tiles(vb, prev_ref, next_ref, coef_ref, out_ref, send=1, group=group, **kwargs)


def outer_rest_kernel(vb, prev_ref, next_ref, coef_ref, out_ref, **kwargs):
    outer_tiles(vb, prev_ref, next_ref, coef_ref, out_ref, send=0, **kwargs)


def blend(front, back, lanes):
    passed = front[3, :, lanes]
    out = [front[k, :, lanes] + passed * back[k, :, lanes] for k in range(3)]
    return out + [passed * back[3, :, lanes]]


def merge_kernel(*refs, depth, step):
    *given, keep_ref, send_ref = refs
    index = lax.axis_index(depth)
    chip = index // 2
    width = keep_ref.shape[2]
    if step == 0:
        in_front, half = index % 2 == 0, (chip ^ (chip // 2)) % 2
    else:
        in_front, half = chip % 2 == 0, chip // 2
    keep_lanes = pl.ds(pl.multiple_of(half * width, width), width)
    send_lanes = pl.ds(pl.multiple_of((1 - half) * width, width), width)
    for mine_first in (True, False):

        @pl.when(in_front == mine_first)
        def _():
            row = 0
            for mine_ref, theirs_ref in zip(given[::2], given[1::2]):
                count = mine_ref.shape[1]
                front, back = (mine_ref, theirs_ref) if mine_first else (theirs_ref, mine_ref)
                for out_ref, lanes in ((send_ref, send_lanes), (keep_ref, keep_lanes)):
                    for k, value in enumerate(blend(front, back, lanes)):
                        out_ref[k, row : row + count, :] = value
                row += count


def final_kernel(*refs, spans, depth):
    out_ref = refs[-1]
    chip = lax.axis_index(depth) // 2
    for mine_first in (True, False):

        @pl.when((chip < 2) == mine_first)
        def _():
            for i, parts in enumerate(spans):
                front, back = (refs[2 * i], refs[2 * i + 1]) if mine_first else (refs[2 * i + 1], refs[2 * i])
                values = blend(front, back, slice(None))
                values[3] = 1.0 - values[3]
                for at, row, count in parts:
                    for k, value in enumerate(values):
                        out_ref[k, row : row + count, :] = value[at : at + count]


def call(body, out_shape, in_specs, args, scratch=(), aliases=None, limit=4, **kwargs):
    single = not isinstance(out_shape, tuple)
    out_specs = VMEM if single else (VMEM,) * len(out_shape)
    return pl.pallas_call(
        functools.partial(body, **kwargs),
        out_shape=out_shape,
        in_specs=in_specs,
        out_specs=out_specs,
        scratch_shapes=scratch,
        input_output_aliases=aliases or {},
        compiler_params=pltpu.CompilerParams(vmem_limit_bytes=limit * 2**20),
    )(*args)


def on_device(volume, palette):
    planes, rows, columns = volume.shape
    groups = lax.axis_size("depth")
    stacks = lax.axis_size("row")
    tiles = columns // LANES
    scale = 4.0 / (planes * groups)

    def ring(value, axis, count, step):
        return lax.ppermute(value, axis, [(i, (i + step) % count) for i in range(count)])

    before = ring(volume[-1], "depth", groups, 1)
    after = ring(volume[0], "depth", groups, -1)
    staged = vmem_shape(tiles + 2, planes, STAGED, LANES)
    strip = vmem_shape(4, SUBLANES, columns)
    edge = vmem_shape(planes, columns)
    to_hbm = lambda value: pltpu.with_memory_space_constraint(value, pltpu.HBM)
    vb, coef, first, top, bottom = call(
        stage_kernel,
        (staged, vmem_shape(palette.size, SUBLANES, LANES), strip, edge, edge),
        [HBM, HBM],
        (to_hbm(volume), to_hbm(palette)),
        scratch=[
            pltpu.SMEM(palette.shape, jnp.float32),
            pltpu.SemaphoreType.DMA((tiles,)),
            pltpu.SemaphoreType.DMA(()),
        ],
        scale=scale,
    )
    above = in_vmem(ring(bottom, "row", stacks, 1))
    below = in_vmem(ring(top, "row", stacks, -1))
    common = dict(scale=scale, planes=planes)
    coef = in_vmem(coef)
    second = call(early_kernel, strip, [VMEM, VMEM], (in_vmem(vb), coef), **common)
    common.update(depth="depth", groups=groups)
    before, after = in_vmem(before), in_vmem(after)
    half = lambda count: vmem_shape(4, count, columns // 2)
    pairs = lambda other: [(i, other(i)) for i in range(groups)]
    partners = [pairs(lambda i: i ^ 1), pairs(lambda i: i ^ 2), pairs(lambda i: groups - 2 - i // 2 * 2 + i % 2)]

    def swap(value, step):
        return lax.ppermute(value, "depth", partners[step])

    def middle(send):
        return call(
            middle_kernel,
            half(16),
            [VMEM] * 6,
            (in_vmem(vb), before, after, in_vmem(first), in_vmem(second), coef),
            send=send,
            **common,
        )

    def outer(vb, edge, behind, group):
        return call(
            outer_kernel,
            (staged, half(8)),
            [VMEM] * 4 + [ANY, VMEM],
            (in_vmem(vb), before, after, edge, behind, coef),
            aliases={0: 0},
            row="row",
            stacks=stacks,
            group=group,
            **common,
        )

    def outer_rest(vb, group):
        return call(outer_rest_kernel, half(8), [VMEM] * 4, (in_vmem(vb), before, after, coef), group=group, **common)

    def merged(given, step):
        channels, _, width = given[0].shape
        shape = (vmem_shape(channels, sum(value.shape[1] for value in given[::2]), width // 2),) * 2
        return call(
            merge_kernel, shape, [VMEM] * len(given), [in_vmem(value) for value in given], depth="depth", step=step
        )

    arrived0 = swap(middle(1), 0)
    kept0 = middle(0)
    behind = kept0
    kept0, send = merged([kept0, arrived0], 0)
    arrived0 = swap(send, 1)
    vb, send = outer(vb, above, behind, 0)
    arrived1 = swap(send, 0)
    kept1 = outer_rest(vb, 0)
    behind = kept1
    kept1, send = merged([kept1, arrived1], 0)
    arrived1 = swap(send, 1)
    vb, send = outer(vb, below, behind, 3)
    arrived2 = swap(send, 0)
    kept01, send = merged([kept0, arrived0, kept1, arrived1], 1)
    arrived01 = swap(send, 2)
    kept2 = outer_rest(vb, 3)
    kept2, send = merged([kept2, arrived2], 0)
    arrived2 = swap(send, 1)
    kept2, send = merged([kept2, arrived2], 1)
    arrived2 = swap(send, 2)
    return call(
        final_kernel,
        jax.ShapeDtypeStruct((4, rows, columns // groups), jnp.float32),
        [VMEM] * 4,
        [in_vmem(value) for value in (kept01, arrived01, kept2, arrived2)],
        spans=(((0, 8, 16), (16, 0, 8)), ((0, 24, 8),)),
        depth="depth",
    )


def solution(mesh):
    return jax.shard_map(
        on_device,
        mesh=mesh,
        in_specs=(P("depth", "row", None), P()),
        out_specs=P(None, "row", "depth"),
        check_vma=False,
    )
```

```python
import functools
import math

import jax
import jax.numpy as jnp
from jax import lax
from jax.experimental import pallas as pl
from jax.experimental.pallas import tpu as pltpu
from jax.sharding import PartitionSpec as P


LANES = 128
SUBLANES = 8
BELOW = 8
STAGED = 48
LOG2E = math.log2(math.e)
TO_Y = 4.0 / 3.0
TO_X = 20.0 / 9.0
AMBIENT = 0.25 / 0.27
AHEAD = 16
VMEM = pl.BlockSpec(memory_space=pltpu.VMEM)
ANY = pl.BlockSpec(memory_space=pl.ANY)
HBM = pl.BlockSpec(memory_space=pltpu.HBM)
SMEM = pl.BlockSpec(memory_space=pltpu.SMEM)


def in_vmem(value):
    return pltpu.with_memory_space_constraint(value, pltpu.VMEM)


def vmem_shape(*shape):
    return pltpu.VMEM(shape, jnp.float32)


def shade_of(dz, dy, dx):
    along = jnp.abs(dz + TO_Y * dy + TO_X * dx)
    square = (dz * dz + 0.16) + (dy * dy + dx * dx)
    return along * lax.rsqrt(square) + AMBIENT


def across(left, here, right):
    lane = lax.broadcasted_iota(jnp.int32, (SUBLANES, LANES), 1)
    after = pltpu.roll(jnp.where(lane == 0, right, here), LANES - 1, 1)
    before = pltpu.roll(jnp.where(lane == LANES - 1, left, here), 1, 1)
    return after - before


def add_bumps(moments, amount, field):
    ratio = jnp.exp2(field * (14 * LOG2E))
    amount = amount * jnp.exp2(field * field * (-49 * LOG2E))
    out = []
    for j, moment in enumerate(moments):
        out.append(amount if moment is None else moment + amount)
        if j + 1 < len(moments):
            amount = amount * ratio
    return out


def contracted(coef_ref, moments):
    bumps = len(moments)
    out = []
    for k in range(3):
        total = moments[0] * coef_ref[k * bumps]
        for j in range(1, bumps):
            total = total + moments[j] * coef_ref[k * bumps + j]
        out.append(total)
    return out


def tile_lanes(c):
    return pl.ds(pl.multiple_of(c * LANES, LANES), LANES)


def gradients(vb, c, z, row, up, down):
    here = vb[c + 1, z, pl.ds(row, 8), :]
    dy = vb[c + 1, z, pl.ds(row + 1, 8), :] - vb[c + 1, z, pl.ds(row - 1, 8), :]
    dx = across(vb[c, z, pl.ds(row, 8), :], here, vb[c + 2, z, pl.ds(row, 8), :])
    if up is None:
        up = vb[c + 1, z + 1, pl.ds(row, 8), :]
    if down is None:
        down = vb[c + 1, z - 1, pl.ds(row, 8), :]
    return here, up - down, dy, dx


def march(vb, c, group, planes, scale, ends=None):
    row = BELOW + group * SUBLANES
    moments = [None] * 8
    total = jnp.zeros((SUBLANES, LANES), jnp.float32)
    passed = jnp.ones((SUBLANES, LANES), jnp.float32)
    for z in range(planes):
        outer = z in (0, planes - 1)
        total = total + vb[c + 1, z, pl.ds(row, 8), :]
        after = jnp.exp2(total * (-scale * LOG2E))
        if not outer or ends is not None:
            down = ends[0] if z == 0 else None
            up = ends[1] if z == planes - 1 else None
            here, dz, dy, dx = gradients(vb, c, z, row, up, down)
            moments = add_bumps(moments, (passed - after) * shade_of(dz, dy, dx), here)
        passed = after
    return moments, passed


def march_ends(vb, c, group, planes, scale, ends, passed):
    row = BELOW + group * SUBLANES
    here, dz, dy, dx = gradients(vb, c, 0, row, None, ends[0])
    amount = 1.0 - jnp.exp2(here * (-scale * LOG2E))
    moments = add_bumps([None] * 8, amount * shade_of(dz, dy, dx), here)
    here, dz, dy, dx = gradients(vb, c, planes - 1, row, ends[1], None)
    amount = passed * (jnp.exp2(here * (scale * LOG2E)) - 1.0)
    return add_bumps(moments, amount * shade_of(dz, dy, dx), here)


def march_early(vb, coef_ref, early_ref, c, planes, scale):
    moments, passed = march(vb, c, 1, planes, scale)
    for k, value in enumerate(contracted(coef_ref, moments) + [passed]):
        early_ref[k, :, tile_lanes(c)] = value


def edge_kernel(volume_ref, *refs):
    *outs, sem = refs
    planes, rows, _ = volume_ref.shape
    sources = [volume_ref.at[:, 0, :], volume_ref.at[:, rows - 1, :], volume_ref.at[0], volume_ref.at[planes - 1]]
    copies = [pltpu.make_async_copy(source, out, sem.at[i]) for i, (source, out) in enumerate(zip(sources, outs))]
    for copy in copies:
        copy.start()
    for copy in copies:
        copy.wait()


def stage_kernel(volume_ref, palette_ref, vb, coef_ref, early_ref, palette, sem, palette_sem, *, scale):
    planes, rows, columns = volume_ref.shape
    tiles = columns // LANES
    bumps = palette_ref.shape[1]

    def copy(c):
        return pltpu.make_async_copy(
            volume_ref.at[:, :, tile_lanes(c)], vb.at[c + 1, :, pl.ds(BELOW, rows), :], sem.at[c]
        )

    weights = pltpu.make_async_copy(palette_ref, palette, palette_sem)
    weights.start()
    for c in range(AHEAD):
        copy(c).start()
    zero = jnp.zeros((planes, rows, LANES), jnp.float32)
    vb[0, :, BELOW : BELOW + rows, :] = zero
    vb[tiles + 1, :, BELOW : BELOW + rows, :] = zero
    weights.wait()
    for k in range(3):
        for j in range(bumps):
            weight = palette[k, j] * jnp.float32(0.27 * math.exp(-j * j))
            coef_ref[k * bumps + j] = jnp.full((SUBLANES, LANES), weight, jnp.float32)

    def arrive(c):
        @pl.when(c < tiles)
        def _():
            copy(c).wait()

        @pl.when(c + AHEAD < tiles)
        def _():
            copy(c + AHEAD).start()

    arrive(0)

    def body(i, _):
        arrive(2 * i + 1)
        arrive(2 * i + 2)
        for c in (2 * i, 2 * i + 1):
            march_early(vb, coef_ref, early_ref, c, planes, scale)
        return 0

    lax.fori_loop(0, tiles // 2, body, 0)


def group_of(chip):
    return (chip ^ (chip // 2)) % 2


def tile_at(place, tiles, parity):
    per_block = tiles // 8
    position = place // per_block
    chip = jnp.where(position < 2, 3 * position, position - 1)
    return (2 * chip + parity) * per_block + place % per_block


def depth_ends(prev_ref, next_ref, index, groups):
    inside_prev = jnp.where(index == 0, 0.0, 1.0)
    inside_next = jnp.where(index == groups - 1, 0.0, 1.0)

    def ends(c, group):
        rows = pl.ds(group * SUBLANES, SUBLANES)
        return prev_ref[rows, tile_lanes(c)] * inside_prev, next_ref[rows, tile_lanes(c)] * inside_next

    return ends


def middle_kernel(vb, prev_ref, next_ref, early_ref, coef_ref, out_ref, *, scale, planes, depth, groups, send):
    tiles = vb.shape[0] - 2
    index = lax.axis_index(depth)
    ends = depth_ends(prev_ref, next_ref, index, groups)
    parity = (index + send) % 2

    def body(m, _):
        for place in (2 * m, 2 * m + 1):
            c = tile_at(place, tiles, parity)
            moments, passed = march(vb, c, 2, planes, scale, ends(c, 2))
            for k, value in enumerate(contracted(coef_ref, moments) + [passed]):
                out_ref[k, 8:16, tile_lanes(place)] = value
            passed = early_ref[3, :, tile_lanes(c)]
            moments = march_ends(vb, c, 1, planes, scale, ends(c, 1), passed)
            for k, color in enumerate(contracted(coef_ref, moments)):
                out_ref[k, 0:8, tile_lanes(place)] = early_ref[k, :, tile_lanes(c)] + color
            out_ref[3, 0:8, tile_lanes(place)] = passed
        return 0

    lax.fori_loop(0, tiles // 4, body, 0)


def outer_tiles(vb, prev_ref, next_ref, coef_ref, out_ref, *, scale, planes, depth, groups, part, group):
    tiles = vb.shape[0] - 2
    index = lax.axis_index(depth)
    ends = depth_ends(prev_ref, next_ref, index, groups)
    parity = (index + (part == 0)) % 2
    mine = group_of(index // 2)
    first = {0: 0, 1: (1 - mine) * (tiles // 4), 2: mine * (tiles // 4)}[part]

    def body(m, _):
        for at in (2 * m, 2 * m + 1):
            c = tile_at(first + at, tiles, parity)
            moments, passed = march(vb, c, group, planes, scale, ends(c, group))
            for k, value in enumerate(contracted(coef_ref, moments) + [passed]):
                out_ref[k, :, tile_lanes(at)] = value
        return 0

    lax.fori_loop(0, out_ref.shape[2] // (2 * LANES), body, 0)


def outer_kernel(vb_in, prev_ref, next_ref, edge_ref, behind_ref, coef_ref, vb, out_ref, *, row, stacks, group, **kwargs):
    tiles, planes = vb.shape[0] - 2, vb.shape[1]
    top = group == 0
    at_end = lax.axis_index(row) == (0 if top else stacks - 1)
    inside = jnp.where(at_end, 0.0, 1.0)
    slot = BELOW - 1 if top else BELOW + 4 * SUBLANES
    flat = vb.reshape(tiles + 2, planes * STAGED, LANES)

    def place(c, _):
        for z in range(0, planes, 8):
            flat[c + 1, pl.ds(z * STAGED + slot, 8, stride=STAGED), :] = edge_ref[z : z + 8, tile_lanes(c)] * inside
        return 0

    lax.fori_loop(0, tiles, place, 0)
    outer_tiles(vb, prev_ref, next_ref, coef_ref, out_ref, part=0, group=group, **kwargs)


def blend(front, back, lanes):
    passed = front[3, :, lanes]
    out = [front[k, :, lanes] + passed * back[k, :, lanes] for k in range(3)]
    return out + [passed * back[3, :, lanes]]


def merge_kernel(*refs, depth, step):
    *given, keep_ref, send_ref = refs
    index = lax.axis_index(depth)
    chip = index // 2
    width = keep_ref.shape[2]
    if step == 0:
        in_front, half = index % 2 == 0, group_of(chip)
    else:
        in_front, half = chip % 2 == 0, chip // 2
    keep_lanes = pl.ds(pl.multiple_of(half * width, width), width)
    send_lanes = pl.ds(pl.multiple_of((1 - half) * width, width), width)
    for mine_first in (True, False):

        @pl.when(in_front == mine_first)
        def _():
            row = 0
            for mine_ref, theirs_ref in zip(given[::2], given[1::2]):
                count = mine_ref.shape[1]
                front, back = (mine_ref, theirs_ref) if mine_first else (theirs_ref, mine_ref)
                for out_ref, lanes in ((send_ref, send_lanes), (keep_ref, keep_lanes)):
                    for k, value in enumerate(blend(front, back, lanes)):
                        out_ref[k, row : row + count, :] = value
                row += count


def fold_kernel(mine_ref, theirs_ref, out_ref, *, depth, send):
    index = lax.axis_index(depth)
    width = out_ref.shape[2]
    group = group_of(index // 2)
    group = 1 - group if send else group
    lanes = pl.ds(pl.multiple_of(group * width, width), width)
    mine, theirs = mine_ref, theirs_ref.at[:, :, lanes]
    for mine_first in (True, False):

        @pl.when((index % 2 == 0) == mine_first)
        def _():
            front, back = (mine, theirs) if mine_first else (theirs, mine)
            for k, value in enumerate(blend(front, back, slice(None))):
                out_ref[k] = value


def final_kernel(*refs, spans, depth):
    out_ref = refs[-1]
    chip = lax.axis_index(depth) // 2
    for mine_first in (True, False):

        @pl.when((chip < 2) == mine_first)
        def _():
            for i, parts in enumerate(spans):
                front, back = (refs[2 * i], refs[2 * i + 1]) if mine_first else (refs[2 * i + 1], refs[2 * i])
                values = blend(front, back, slice(None))
                values[3] = 1.0 - values[3]
                for at, row, count in parts:
                    for k, value in enumerate(values):
                        out_ref[k, row : row + count, :] = value[at : at + count]


def call(body, out_shape, in_specs, args, scratch=(), aliases=None, limit=4, **kwargs):
    single = not isinstance(out_shape, tuple)
    out_specs = VMEM if single else (VMEM,) * len(out_shape)
    return pl.pallas_call(
        functools.partial(body, **kwargs),
        out_shape=out_shape,
        in_specs=in_specs,
        out_specs=out_specs,
        scratch_shapes=scratch,
        input_output_aliases=aliases or {},
        compiler_params=pltpu.CompilerParams(vmem_limit_bytes=limit * 2**20),
    )(*args)


def on_device(volume, palette):
    planes, rows, columns = volume.shape
    groups = lax.axis_size("depth")
    stacks = lax.axis_size("row")
    tiles = columns // LANES
    scale = 4.0 / (planes * groups)

    def ring(value, axis, count, step):
        return lax.ppermute(value, axis, [(i, (i + step) % count) for i in range(count)])

    staged = vmem_shape(tiles + 2, planes, STAGED, LANES)
    strip = vmem_shape(4, SUBLANES, columns)
    to_hbm = lambda value: pltpu.with_memory_space_constraint(value, pltpu.HBM)
    volume = to_hbm(volume)
    low, high, front, back = call(
        edge_kernel,
        (vmem_shape(planes, columns),) * 2 + (vmem_shape(rows, columns),) * 2,
        [HBM],
        (volume,),
        scratch=[pltpu.SemaphoreType.DMA((4,))],
    )
    above = in_vmem(ring(high, "row", stacks, 1))
    below = in_vmem(ring(low, "row", stacks, -1))
    before = in_vmem(ring(back, "depth", groups, 1))
    after = in_vmem(ring(front, "depth", groups, -1))
    vb, coef, early = call(
        stage_kernel,
        (staged, vmem_shape(palette.size, SUBLANES, LANES), strip),
        [HBM, HBM],
        (volume, to_hbm(palette)),
        scratch=[
            pltpu.SMEM(palette.shape, jnp.float32),
            pltpu.SemaphoreType.DMA((tiles,)),
            pltpu.SemaphoreType.DMA(()),
        ],
        scale=scale,
    )
    coef = in_vmem(coef)
    common = dict(scale=scale, planes=planes, depth="depth", groups=groups)
    pairs = lambda other: [(i, other(i)) for i in range(groups)]
    partners = [pairs(lambda i: i ^ 1), pairs(lambda i: i ^ 2), pairs(lambda i: groups - 2 - i // 2 * 2 + i % 2)]

    def swap(value, step):
        return in_vmem(lax.ppermute(value, "depth", partners[step]))

    def middle(send):
        return call(
            middle_kernel,
            vmem_shape(4, 16, columns // 2),
            [VMEM] * 5,
            (in_vmem(vb), before, after, in_vmem(early), coef),
            send=send,
            **common,
        )

    def outer_first(vb, edge, behind, group):
        return call(
            outer_kernel,
            (staged, vmem_shape(4, 8, columns // 2)),
            [VMEM] * 4 + [ANY, VMEM],
            (in_vmem(vb), before, after, edge, behind, coef),
            aliases={0: 0},
            row="row",
            stacks=stacks,
            group=group,
            **common,
        )

    def outer(vb, group, part):
        return call(
            outer_tiles,
            vmem_shape(4, 8, columns // 4),
            [VMEM] * 4,
            (in_vmem(vb), before, after, coef),
            group=group,
            part=part,
            **common,
        )

    def fold(mine, theirs, send):
        return call(fold_kernel, vmem_shape(*mine.shape), [VMEM] * 2, (in_vmem(mine), theirs), depth="depth", send=send)

    def merged(given, step):
        channels, _, width = given[0].shape
        shape = (vmem_shape(channels, sum(value.shape[1] for value in given[::2]), width // 2),) * 2
        return call(
            merge_kernel, shape, [VMEM] * len(given), [in_vmem(value) for value in given], depth="depth", step=step
        )

    arrived0 = swap(middle(1), 0)
    behind = middle(0)
    kept0, send = merged([behind, arrived0], 0)
    arrived0 = swap(send, 1)
    vb, send = outer_first(vb, above, behind, 0)
    partner1 = swap(send, 0)
    behind = outer(vb, 0, 1)
    arrived1 = swap(fold(behind, partner1, 1), 1)
    vb, send = outer_first(vb, below, behind, 3)
    partner2 = swap(send, 0)
    arrived2 = swap(fold(outer(vb, 3, 1), partner2, 1), 1)
    kept1 = fold(outer(vb, 0, 2), partner1, 0)
    kept01, send = merged([kept0, arrived0, kept1, arrived1], 1)
    arrived01 = swap(send, 2)
    kept2 = fold(outer(vb, 3, 2), partner2, 0)
    kept2, send = merged([kept2, arrived2], 1)
    arrived2 = swap(send, 2)
    return call(
        final_kernel,
        jax.ShapeDtypeStruct((4, rows, columns // groups), jnp.float32),
        [VMEM] * 4,
        [in_vmem(value) for value in (kept01, arrived01, kept2, arrived2)],
        spans=(((0, 8, 16), (16, 0, 8)), ((0, 24, 8),)),
        depth="depth",
    )


def solution(mesh):
    return jax.shard_map(
        on_device,
        mesh=mesh,
        in_specs=(P("depth", "row", None), P()),
        out_specs=P(None, "row", "depth"),
        check_vma=False,
    )
```

```python
import functools
import math

import jax
import jax.numpy as jnp
from jax import lax
from jax.experimental import pallas as pl
from jax.experimental.pallas import tpu as pltpu
from jax.sharding import PartitionSpec as P


LANES = 128
SUBLANES = 8
BELOW = 8
STAGED = 48
LOG2E = math.log2(math.e)
TO_Y = 4.0 / 3.0
TO_X = 20.0 / 9.0
AMBIENT = 0.25 / 0.27
AHEAD = 16
VMEM = pl.BlockSpec(memory_space=pltpu.VMEM)
ANY = pl.BlockSpec(memory_space=pl.ANY)
HBM = pl.BlockSpec(memory_space=pltpu.HBM)
SMEM = pl.BlockSpec(memory_space=pltpu.SMEM)


def in_vmem(value):
    return pltpu.with_memory_space_constraint(value, pltpu.VMEM)


def vmem_shape(*shape):
    return pltpu.VMEM(shape, jnp.float32)


def shade_of(dz, dy, dx):
    along = jnp.abs(dz + TO_Y * dy + TO_X * dx)
    square = (dz * dz + 0.16) + (dy * dy + dx * dx)
    return along * lax.rsqrt(square) + AMBIENT


def across(left, here, right):
    lane = lax.broadcasted_iota(jnp.int32, (SUBLANES, LANES), 1)
    after = pltpu.roll(jnp.where(lane == 0, right, here), LANES - 1, 1)
    before = pltpu.roll(jnp.where(lane == LANES - 1, left, here), 1, 1)
    return after - before


def add_bumps(moments, amount, field):
    ratio = jnp.exp2(field * (14 * LOG2E))
    amount = amount * jnp.exp2(field * field * (-49 * LOG2E))
    out = []
    for j, moment in enumerate(moments):
        out.append(amount if moment is None else moment + amount)
        if j + 1 < len(moments):
            amount = amount * ratio
    return out


def contracted(coef_ref, moments):
    bumps = len(moments)
    out = []
    for k in range(3):
        total = moments[0] * coef_ref[k * bumps]
        for j in range(1, bumps):
            total = total + moments[j] * coef_ref[k * bumps + j]
        out.append(total)
    return out


def tile_lanes(c):
    return pl.ds(pl.multiple_of(c * LANES, LANES), LANES)


def gradients(vb, c, z, row, up, down):
    here = vb[c + 1, z, pl.ds(row, 8), :]
    dy = vb[c + 1, z, pl.ds(row + 1, 8), :] - vb[c + 1, z, pl.ds(row - 1, 8), :]
    dx = across(vb[c, z, pl.ds(row, 8), :], here, vb[c + 2, z, pl.ds(row, 8), :])
    if up is None:
        up = vb[c + 1, z + 1, pl.ds(row, 8), :]
    if down is None:
        down = vb[c + 1, z - 1, pl.ds(row, 8), :]
    return here, up - down, dy, dx


def march(vb, c, group, planes, scale, ends=None):
    row = BELOW + group * SUBLANES
    moments = [None] * 8
    total = jnp.zeros((SUBLANES, LANES), jnp.float32)
    passed = jnp.ones((SUBLANES, LANES), jnp.float32)
    for z in range(planes):
        outer = z in (0, planes - 1)
        total = total + vb[c + 1, z, pl.ds(row, 8), :]
        after = jnp.exp2(total * (-scale * LOG2E))
        if not outer or ends is not None:
            down = ends[0] if z == 0 else None
            up = ends[1] if z == planes - 1 else None
            here, dz, dy, dx = gradients(vb, c, z, row, up, down)
            moments = add_bumps(moments, (passed - after) * shade_of(dz, dy, dx), here)
        passed = after
    return moments, passed


def march_ends(vb, c, group, planes, scale, ends, passed):
    row = BELOW + group * SUBLANES
    here, dz, dy, dx = gradients(vb, c, 0, row, None, ends[0])
    amount = 1.0 - jnp.exp2(here * (-scale * LOG2E))
    moments = add_bumps([None] * 8, amount * shade_of(dz, dy, dx), here)
    here, dz, dy, dx = gradients(vb, c, planes - 1, row, ends[1], None)
    amount = passed * (jnp.exp2(here * (scale * LOG2E)) - 1.0)
    return add_bumps(moments, amount * shade_of(dz, dy, dx), here)


def march_early(vb, coef_ref, early_ref, c, planes, scale):
    moments, passed = march(vb, c, 1, planes, scale)
    for k, value in enumerate(contracted(coef_ref, moments) + [passed]):
        early_ref[k, :, tile_lanes(c)] = value


def edge_kernel(volume_ref, *refs):
    *outs, sem = refs
    planes, rows, _ = volume_ref.shape
    sources = [volume_ref.at[:, 0, :], volume_ref.at[:, rows - 1, :], volume_ref.at[0], volume_ref.at[planes - 1]]
    copies = [pltpu.make_async_copy(source, out, sem.at[i]) for i, (source, out) in enumerate(zip(sources, outs))]
    for copy in copies:
        copy.start()
    for copy in copies:
        copy.wait()


def stage_kernel(volume_ref, palette_ref, vb, coef_ref, early_ref, palette, sem, palette_sem, *, scale):
    planes, rows, columns = volume_ref.shape
    tiles = columns // LANES
    bumps = palette_ref.shape[1]

    def copy(c):
        return pltpu.make_async_copy(
            volume_ref.at[:, :, tile_lanes(c)], vb.at[c + 1, :, pl.ds(BELOW, rows), :], sem.at[c]
        )

    weights = pltpu.make_async_copy(palette_ref, palette, palette_sem)
    weights.start()
    for c in range(AHEAD):
        copy(c).start()
    zero = jnp.zeros((planes, rows, LANES), jnp.float32)
    vb[0, :, BELOW : BELOW + rows, :] = zero
    vb[tiles + 1, :, BELOW : BELOW + rows, :] = zero
    weights.wait()
    for k in range(3):
        for j in range(bumps):
            weight = palette[k, j] * jnp.float32(0.27 * math.exp(-j * j))
            coef_ref[k * bumps + j] = jnp.full((SUBLANES, LANES), weight, jnp.float32)

    def arrive(c):
        @pl.when(c < tiles)
        def _():
            copy(c).wait()

        @pl.when(c + AHEAD < tiles)
        def _():
            copy(c + AHEAD).start()

    arrive(0)

    def body(i, _):
        arrive(2 * i + 1)
        arrive(2 * i + 2)
        for c in (2 * i, 2 * i + 1):
            march_early(vb, coef_ref, early_ref, c, planes, scale)
        return 0

    lax.fori_loop(0, tiles // 2, body, 0)


def group_of(chip):
    return (chip ^ (chip // 2)) % 2


def tile_at(place, tiles, parity):
    per_block = tiles // 8
    position = place // per_block
    chip = jnp.where(position < 2, 3 * position, position - 1)
    return (2 * chip + parity) * per_block + place % per_block


def depth_ends(prev_ref, next_ref, index, groups):
    inside_prev = jnp.where(index == 0, 0.0, 1.0)
    inside_next = jnp.where(index == groups - 1, 0.0, 1.0)

    def ends(c, group):
        rows = pl.ds(group * SUBLANES, SUBLANES)
        return prev_ref[rows, tile_lanes(c)] * inside_prev, next_ref[rows, tile_lanes(c)] * inside_next

    return ends


def first_place(index, tiles, part):
    mine = group_of(index // 2)
    half = index // 4 if part == 3 else 1 - index // 4
    quarter = tiles // 4
    first = {0: 0, 1: (1 - mine) * quarter}.get(part, mine * quarter + half * (quarter // 2))
    return first, (index + (part == 0)) % 2


def width_of(columns, part):
    return columns // (2, 4, 8, 8)[part]


def middle_kernel(vb, prev_ref, next_ref, early_ref, coef_ref, out_ref, *, scale, planes, depth, groups, part):
    tiles = vb.shape[0] - 2
    index = lax.axis_index(depth)
    ends = depth_ends(prev_ref, next_ref, index, groups)
    first, parity = first_place(index, tiles, part)

    def body(m, _):
        for at in (2 * m, 2 * m + 1):
            c = tile_at(first + at, tiles, parity)
            moments, passed = march(vb, c, 2, planes, scale, ends(c, 2))
            for k, value in enumerate(contracted(coef_ref, moments) + [passed]):
                out_ref[k, 8:16, tile_lanes(at)] = value
            passed = early_ref[3, :, tile_lanes(c)]
            moments = march_ends(vb, c, 1, planes, scale, ends(c, 1), passed)
            for k, color in enumerate(contracted(coef_ref, moments)):
                out_ref[k, 0:8, tile_lanes(at)] = early_ref[k, :, tile_lanes(c)] + color
            out_ref[3, 0:8, tile_lanes(at)] = passed
        return 0

    lax.fori_loop(0, out_ref.shape[2] // (2 * LANES), body, 0)


def outer_tiles(vb, prev_ref, next_ref, coef_ref, out_ref, *, scale, planes, depth, groups, part, group):
    tiles = vb.shape[0] - 2
    index = lax.axis_index(depth)
    ends = depth_ends(prev_ref, next_ref, index, groups)
    first, parity = first_place(index, tiles, part)

    def body(m, _):
        for at in (2 * m, 2 * m + 1):
            c = tile_at(first + at, tiles, parity)
            moments, passed = march(vb, c, group, planes, scale, ends(c, group))
            for k, value in enumerate(contracted(coef_ref, moments) + [passed]):
                out_ref[k, :, tile_lanes(at)] = value
        return 0

    lax.fori_loop(0, out_ref.shape[2] // (2 * LANES), body, 0)


def outer_kernel(vb_in, prev_ref, next_ref, edge_ref, behind_ref, coef_ref, vb, out_ref, *, row, stacks, group, **kwargs):
    tiles, planes = vb.shape[0] - 2, vb.shape[1]
    top = group == 0
    at_end = lax.axis_index(row) == (0 if top else stacks - 1)
    inside = jnp.where(at_end, 0.0, 1.0)
    slot = BELOW - 1 if top else BELOW + 4 * SUBLANES
    flat = vb.reshape(tiles + 2, planes * STAGED, LANES)

    def place(c, _):
        for z in range(0, planes, 8):
            flat[c + 1, pl.ds(z * STAGED + slot, 8, stride=STAGED), :] = edge_ref[z : z + 8, tile_lanes(c)] * inside
        return 0

    lax.fori_loop(0, tiles, place, 0)
    outer_tiles(vb, prev_ref, next_ref, coef_ref, out_ref, part=0, group=group, **kwargs)


def blend(front, back, lanes):
    passed = front[3, :, lanes]
    out = [front[k, :, lanes] + passed * back[k, :, lanes] for k in range(3)]
    return out + [passed * back[3, :, lanes]]


def fold_kernel(mine_ref, theirs_ref, out_ref, *, depth):
    index = lax.axis_index(depth)
    width = out_ref.shape[2]
    lanes = pl.ds(pl.multiple_of((1 - group_of(index // 2)) * width, width), width)
    mine, theirs = mine_ref, theirs_ref.at[:, :, lanes]
    for mine_first in (True, False):

        @pl.when((index % 2 == 0) == mine_first)
        def _():
            front, back = (mine, theirs) if mine_first else (theirs, mine)
            for k, value in enumerate(blend(front, back, slice(None))):
                out_ref[k] = value


def block_kernel(*refs, depth, part):
    *given, out_ref = refs
    index = lax.axis_index(depth)
    chip = index // 2
    width = out_ref.shape[2]
    half = chip // 2 if part == 3 else 1 - chip // 2
    lanes = lambda block: pl.ds(pl.multiple_of(block * width, width), width)
    row = 0
    for mine_ref, core_ref, chip_ref in zip(given[::3], given[1::3], given[2::3]):
        rows = pl.ds(row, mine_ref.shape[1])
        out = out_ref.at[:, rows, :]
        core, beside = core_ref.at[:, :, lanes(2 * group_of(chip) + half)], chip_ref.at[:, :, lanes(half)]
        for theirs, mine, at in ((core, mine_ref, index), (beside, out, chip)):
            for mine_first in (True, False):

                @pl.when((at % 2 == 0) == mine_first)
                def _():
                    front, back = (mine, theirs) if mine_first else (theirs, mine)
                    for k, value in enumerate(blend(front, back, slice(None))):
                        out[k] = value

        row += mine_ref.shape[1]


def final_kernel(mine_ref, *refs, spans, depth):
    *given, out_ref = refs
    chip = lax.axis_index(depth) // 2
    for mine_first in (True, False):

        @pl.when((chip < 2) == mine_first)
        def _():
            first = 0
            for theirs, parts in zip(given, spans):
                mine = mine_ref.at[:, pl.ds(first, theirs.shape[1]), :]
                front, back = (mine, theirs) if mine_first else (theirs, mine)
                values = blend(front, back, slice(None))
                values[3] = 1.0 - values[3]
                for at, row, count in parts:
                    for k, value in enumerate(values):
                        out_ref[k, row : row + count, :] = value[at : at + count]
                first += theirs.shape[1]


def call(body, out_shape, in_specs, args, scratch=(), aliases=None, limit=4, **kwargs):
    single = not isinstance(out_shape, tuple)
    out_specs = VMEM if single else (VMEM,) * len(out_shape)
    return pl.pallas_call(
        functools.partial(body, **kwargs),
        out_shape=out_shape,
        in_specs=in_specs,
        out_specs=out_specs,
        scratch_shapes=scratch,
        input_output_aliases=aliases or {},
        compiler_params=pltpu.CompilerParams(vmem_limit_bytes=limit * 2**20),
    )(*args)


def on_device(volume, palette):
    planes, rows, columns = volume.shape
    groups = lax.axis_size("depth")
    stacks = lax.axis_size("row")
    tiles = columns // LANES
    scale = 4.0 / (planes * groups)

    def ring(value, axis, count, step):
        return lax.ppermute(value, axis, [(i, (i + step) % count) for i in range(count)])

    staged = vmem_shape(tiles + 2, planes, STAGED, LANES)
    strip = vmem_shape(4, SUBLANES, columns)
    to_hbm = lambda value: pltpu.with_memory_space_constraint(value, pltpu.HBM)
    volume = to_hbm(volume)
    low, high, front, back = call(
        edge_kernel,
        (vmem_shape(planes, columns),) * 2 + (vmem_shape(rows, columns),) * 2,
        [HBM],
        (volume,),
        scratch=[pltpu.SemaphoreType.DMA((4,))],
    )
    above = in_vmem(ring(high, "row", stacks, 1))
    below = in_vmem(ring(low, "row", stacks, -1))
    before = in_vmem(ring(back, "depth", groups, 1))
    after = in_vmem(ring(front, "depth", groups, -1))
    vb, coef, early = call(
        stage_kernel,
        (staged, vmem_shape(palette.size, SUBLANES, LANES), strip),
        [HBM, HBM],
        (volume, to_hbm(palette)),
        scratch=[
            pltpu.SMEM(palette.shape, jnp.float32),
            pltpu.SemaphoreType.DMA((tiles,)),
            pltpu.SemaphoreType.DMA(()),
        ],
        scale=scale,
    )
    coef = in_vmem(coef)
    common = dict(scale=scale, planes=planes, depth="depth", groups=groups)
    pairs = lambda other: [(i, other(i)) for i in range(groups)]
    partners = [pairs(lambda i: i ^ 1), pairs(lambda i: i ^ 2), pairs(lambda i: groups - 2 - i // 2 * 2 + i % 2)]

    def swap(value, step):
        return in_vmem(lax.ppermute(value, "depth", partners[step]))

    def middle(part, vb):
        return in_vmem(
            call(
                middle_kernel,
                vmem_shape(4, 16, width_of(columns, part)),
                [VMEM] * 5,
                (in_vmem(vb), before, after, in_vmem(early), coef),
                part=part,
                **common,
            )
        )

    def outer_first(vb, edge, behind, group):
        return call(
            outer_kernel,
            (staged, vmem_shape(4, 8, columns // 2)),
            [VMEM] * 4 + [ANY, VMEM],
            (in_vmem(vb), before, after, edge, behind, coef),
            aliases={0: 0},
            row="row",
            stacks=stacks,
            group=group,
            **common,
        )

    def outer(vb, group, part):
        return in_vmem(
            call(
                outer_tiles,
                vmem_shape(4, 8, width_of(columns, part)),
                [VMEM] * 4,
                (in_vmem(vb), before, after, coef),
                group=group,
                part=part,
                **common,
            )
        )

    def fold(mine, theirs):
        return call(fold_kernel, vmem_shape(*mine.shape), [VMEM] * 2, (mine, theirs), depth="depth")

    def blocks(given, part):
        count = sum(value.shape[1] for value in given[::3])
        return call(
            block_kernel, vmem_shape(4, count, columns // groups), [VMEM] * len(given), given, depth="depth", part=part
        )

    core0 = swap(middle(0, vb), 0)
    behind = middle(1, vb)
    chip0 = swap(fold(behind, core0), 1)
    vb, send = outer_first(vb, above, behind, 0)
    core1 = swap(send, 0)
    behind = outer(vb, 0, 1)
    chip1 = swap(fold(behind, core1), 1)
    vb, send = outer_first(vb, below, behind, 3)
    core2 = swap(send, 0)
    chip2 = swap(fold(outer(vb, 3, 1), core2), 1)
    far01 = swap(blocks([middle(2, vb), core0, chip0, outer(vb, 0, 2), core1, chip1], 2), 2)
    middle_mine = middle(3, vb)
    far2 = swap(blocks([outer(vb, 3, 2), core2, chip2], 2), 2)
    mine = [middle_mine, core0, chip0, outer(vb, 0, 3), core1, chip1, outer(vb, 3, 3), core2, chip2]
    return call(
        final_kernel,
        jax.ShapeDtypeStruct((4, rows, columns // groups), jnp.float32),
        [VMEM] * 3,
        (in_vmem(blocks(mine, 3)), far01, far2),
        spans=(((0, 8, 16), (16, 0, 8)), ((0, 24, 8),)),
        depth="depth",
    )


def solution(mesh):
    return jax.shard_map(
        on_device,
        mesh=mesh,
        in_specs=(P("depth", "row", None), P()),
        out_specs=P(None, "row", "depth"),
        check_vma=False,
    )
```
